128 devices in a mesh: exp: 16 (over y, z_hi, core), row: 8 (over z_lo, x).
Axes of the slice: x: 4, y: 4, z: 4 (z_hi: 2, z_lo: 2; z = z_hi * 2 + z_lo), core: 2. Of those that a mesh axis runs over, the one named last changes fastest.
Arguments:
- exposures: bfloat16 [16, 39, 128, 2048], P('exp', None, 'row'), may hold values from -6 to 6
- fake_flux: float32 [16, 39, 16], P('exp'), may hold values from -24 to 24
- fake_rows: int32 [16], replicated, may hold values from 0 to 127
- fake_cols: int32 [16], replicated, may hold values from 0 to 2047
- kernel_taps: float32 [39, 16], replicated, may hold values from -0.25 to 0.5
- band_offsets: int32 [39], replicated, may hold values from -12 to -4, as said below
- analysis: bfloat16 [8, 39], replicated, may hold values from -1 to 1
- spectral_basis: bfloat16 [39, 8], replicated, may hold values from -2 to 2
- exposure_weights: float32 [16], replicated, may hold values from -4 to 4
Outputs:
- detection_map: float32 [39, 128, 2048], P(None, 'exp', 'row')
The draws below stay inside these ranges and needn't reach their ends.
Inputs may be any that keep to these rules, and one draw needn't show every extreme that they name: `band_offsets`: each channel's offset lies in a range such that every output pixel reads pixels at most 12 away; some channel has the smallest offset and some the largest.
All inputs are finite; a program needn't handle non-finite values.
Results may differ from the reference program's by a relative error of at most 0.0065.
Values may be sent and summed in bfloat16 or wider, within the bound.
No kernel may reach another device: no remote copies, remote signals or barrier semaphores. Data moves between devices by JAX's collectives and lax.ppermute only.
A program may use at most 128 MiB of HBM per device.

```python
import jax
import jax.numpy as jnp
from jax import lax

C = 39
K = 8
TAPS = 16
REACH = 12
W = 2048
NF = 16
E = 16
H = 128


def draw_band_offsets(key, part):
    base = jax.random.randint(jax.random.fold_in(key, 11), (C,), -REACH, REACH - TAPS + 1)
    order = jax.random.permutation(jax.random.fold_in(key, 12), C)
    base = base.at[order[0]].set(-REACH)
    base = base.at[order[1]].set(REACH - TAPS)
    return base.astype(jnp.int32)


def touch_ends(values, stream_key, low, top_value):
    spot = [jax.random.randint(jax.random.fold_in(stream_key, axis), (), 0, length) for axis, length in enumerate(values.shape)]
    widest = values.shape.index(max(values.shape))
    next_to = spot[:widest] + [(spot[widest] + 1) % values.shape[widest]] + spot[widest + 1:]
    return values.at[tuple(spot)].set(low).at[tuple(next_to)].set(top_value)


def block_levels(own_key, shape, pieces, low, high):
    loudness, own = 1.0, jax.random.fold_in(own_key, 6)
    for position, blocks in pieces:
        heights = jnp.exp(jax.random.uniform(jax.random.fold_in(own, position), (blocks,), jnp.float32, low / len(pieces), high / len(pieces)))
        loudness = loudness * jnp.repeat(heights, shape[position] // blocks).reshape([-1 if axis == position else 1 for axis in range(len(shape))])
    return loudness


def centred(stream_key, extent, width, limit, split=(), held_as=jnp.bfloat16):
    entries = width * jax.random.normal(stream_key, extent, jnp.float32)
    if split:
        entries = entries * block_levels(stream_key, extent, split, -0.22, 0.18)
    return jnp.clip(entries, -limit, limit).astype(held_as)


def setup_inputs(seed: int = 0) -> dict:
    splits = jax.random.split(jax.random.key(seed), 10)
    exposures = centred(splits[0], (E, C, H, W), 1.0, 6.0, ((0, 16), (2, 8)))
    fake_flux = centred(splits[1], (E, C, NF), 4.0, 24.0, ((0, 16),), jnp.float32)
    fake_rows = touch_ends(jax.random.randint(splits[2], (NF,), 0, H), jax.random.fold_in(splits[2], 1), 0, H - 1).astype(jnp.int32)
    fake_cols = touch_ends(jax.random.randint(splits[3], (NF,), 0, W), jax.random.fold_in(splits[3], 1), 0, W - 1).astype(jnp.int32)
    kernel_taps = jnp.clip(jax.random.uniform(splits[4], (C, TAPS), jnp.float32, -0.25, 0.5), -0.25, 0.5)
    band_offsets = draw_band_offsets(jax.random.fold_in(splits[9], 71), 0)
    analysis = centred(splits[6], (K, C), C ** -0.5, 1.0)
    spectral_basis = centred(splits[7], (C, K), K ** -0.5, 2.0)
    exposure_weights = centred(splits[8], (E,), 1.0, 4.0, (), jnp.float32)
    return {"exposures": exposures, "fake_flux": fake_flux, "fake_rows": fake_rows, "fake_cols": fake_cols, "kernel_taps": kernel_taps, "band_offsets": band_offsets, "analysis": analysis, "spectral_basis": spectral_basis, "exposure_weights": exposure_weights}


def resample(field, tap_values, offsets, axis):
    length = field.shape[axis]
    widths = [(0, 0)] * 3
    widths[axis] = (REACH, REACH)
    padded = jnp.pad(field, widths)

    def one_channel(channel, offset, weights):
        total = jnp.zeros(channel.shape[:axis - 1] + (length,) + channel.shape[axis:], channel.dtype)
        for tap_index in range(TAPS):
            start = (REACH + offset + tap_index).astype(jnp.int32)
            piece = lax.dynamic_slice_in_dim(channel, start, length, axis - 1)
            total = total + weights[tap_index] * piece
        return total
    return jax.vmap(one_channel)(padded, offsets, tap_values)

def reference(exposures, fake_flux, fake_rows, fake_cols, kernel_taps, band_offsets, analysis, spectral_basis, exposure_weights):
    tap_values = lax.optimization_barrier(kernel_taps.astype(jnp.bfloat16)).astype(jnp.float32)
    row_hits = (fake_rows[:, None] == jnp.arange(H, dtype=jnp.int32)[None, :]).astype(jnp.float32)
    col_hits = (fake_cols[:, None] == jnp.arange(W, dtype=jnp.int32)[None, :]).astype(jnp.float32)

    def one_exposure(pair):
        frame, flux = pair
        added = jnp.einsum('cf,fh,fw->chw', flux, row_hits, col_hits, precision=lax.Precision.HIGHEST)
        injected = (frame.astype(jnp.float32) + added).astype(jnp.bfloat16)
        first = resample(injected.astype(jnp.float32), tap_values, band_offsets, 2).astype(jnp.bfloat16)
        second = resample(first.astype(jnp.float32), tap_values, band_offsets, 1).astype(jnp.bfloat16)
        coefficients = jnp.einsum('kc,chw->khw', analysis.astype(jnp.float32), second.astype(jnp.float32)).astype(jnp.bfloat16)
        model = jnp.einsum('ck,khw->chw', spectral_basis.astype(jnp.float32), coefficients.astype(jnp.float32))
        return (second.astype(jnp.float32) - model).astype(jnp.bfloat16)
    residual = lax.map(one_exposure, (exposures, fake_flux))
    count = residual.shape[0]

    def one_channel(channel):
        values = channel.astype(jnp.float32)
        mean_level = lax.optimization_barrier(jnp.mean(values, axis=0))
        deviation = values - mean_level
        spread = lax.optimization_barrier(jnp.mean(deviation * deviation, axis=0)) + 1e-05
        weighted = jnp.einsum('e,ehw->hw', exposure_weights, deviation, precision=lax.Precision.HIGHEST)
        return weighted / jnp.sqrt(count * spread)
    return lax.map(one_channel, jnp.moveaxis(residual, 1, 0))
```

```python
import jax
import jax.numpy as jnp
from jax import lax
from jax.experimental import pallas as pl
from jax.experimental.pallas import tpu as pltpu
from jax.sharding import PartitionSpec as P

BLOCK = 256
HALF = 128
NEAR = 64
VMEM = pl.BlockSpec(memory_space=pltpu.VMEM)
SMEM = pl.BlockSpec(memory_space=pltpu.SMEM)


def circulant(taps_ref, offsets_ref, channel, sign):
    lane = lax.broadcasted_iota(jnp.int32, (8, HALF), 1)
    signed = jnp.where(lane < NEAR, lane, lane - HALF)
    place = sign * signed - offsets_ref[channel]
    values = jnp.zeros((8, HALF), jnp.float32)
    for tap_index in range(taps_ref.shape[1]):
        values = jnp.where(place == tap_index, taps_ref[channel, tap_index], values)
    rows = jnp.concatenate([values] * (HALF // 8), axis=0)
    return pltpu.roll(rows, 0, 1, stride=1, stride_axis=0)


def distances():
    inner = lax.broadcasted_iota(jnp.int32, (HALF, HALF), 0)
    outer = lax.broadcasted_iota(jnp.int32, (HALF, HALF), 1)
    return outer - inner


def columns_kernel(
    rows_ref, cols_ref, offsets_ref, taps_ref, flux_ref, frames_ref, sent_ref, held_ref
):
    channels, local_rows, width = frames_ref.shape
    pieces = width // BLOCK
    row_start = lax.axis_index("row") * local_rows
    held_ref[...] = frames_ref[...]
    count = rows_ref.shape[0]

    def inject(which, carry):
        local = rows_ref[which] - row_start
        column = cols_ref[which]
        first = jnp.int32(1)
        for other in range(count):
            same = (rows_ref[other] == rows_ref[which]) & (cols_ref[other] == column)
            first = jnp.where(same & (other < which), 0, first)

        @pl.when((local >= 0) & (local < local_rows) & (first == 1))
        def _():
            start = pl.multiple_of((column // HALF) * HALF, HALF)
            row_ids = lax.broadcasted_iota(jnp.int32, (local_rows, HALF), 0)
            col_ids = lax.broadcasted_iota(jnp.int32, (local_rows, HALF), 1)
            hit = (row_ids == local) & (col_ids == column - start)

            def one(channel, inner):
                total = jnp.float32(0.0)
                for other in range(count):
                    same = (rows_ref[other] == rows_ref[which]) & (cols_ref[other] == column)
                    total = total + jnp.where(same, flux_ref[0, channel, other], 0.0)
                tile = held_ref[channel, :, pl.ds(start, HALF)].astype(jnp.float32)
                held_ref[channel, :, pl.ds(start, HALF)] = jnp.where(
                    hit, tile + total, tile
                ).astype(jnp.bfloat16)
                return inner

            lax.fori_loop(0, channels, one, 0)

        return carry

    lax.fori_loop(0, count, inject, 0)
    gap = distances()
    empty = jnp.zeros((HALF, HALF), jnp.bfloat16)
    edge = jnp.zeros((local_rows, HALF), jnp.bfloat16)

    def resample(channel, carry):
        ring = circulant(taps_ref, offsets_ref, channel, -1)
        near = jnp.where(jnp.abs(gap) < NEAR, ring, 0.0).astype(jnp.bfloat16)
        after = jnp.where(gap >= NEAR, ring, 0.0).astype(jnp.bfloat16)
        before = jnp.where(gap <= -NEAR, ring, 0.0).astype(jnp.bfloat16)
        weights = jnp.concatenate(
            [
                jnp.concatenate([near, before], axis=1),
                jnp.concatenate([after, near], axis=1),
                jnp.concatenate([empty, after], axis=1),
                jnp.concatenate([before, empty], axis=1),
            ],
            axis=0,
        )
        values = held_ref[channel]
        lines = []
        for piece in range(pieces):
            start = piece * BLOCK
            follow = values[:, start + BLOCK : start + BLOCK + HALF] if piece < pieces - 1 else edge
            lead = values[:, start - HALF : start] if piece > 0 else edge
            lines.append(
                jnp.concatenate([values[:, start : start + BLOCK], follow, lead], axis=1)
            )
        result = jnp.dot(
            jnp.concatenate(lines, axis=0), weights, preferred_element_type=jnp.float32
        ).astype(jnp.bfloat16)
        for piece in range(pieces):
            sent_ref[piece, channel] = result[piece * local_rows : (piece + 1) * local_rows]
        return carry

    lax.fori_loop(0, channels, resample, 0)


def rows_kernel(
    offsets_ref, taps_ref, analysis_ref, basis_ref, columns_ref, sent_ref, resampled_ref
):
    parts, channels, part_rows, width = columns_ref.shape
    rows = parts * part_rows
    gap = distances()

    def resample(channel, carry):
        ring = circulant(taps_ref, offsets_ref, channel, 1)
        near = jnp.where(jnp.abs(gap) < NEAR, ring, 0.0).astype(jnp.bfloat16)
        values = columns_ref[:, channel].reshape(rows, width)
        resampled_ref[channel] = jnp.dot(
            near, values, preferred_element_type=jnp.float32
        ).astype(jnp.bfloat16)
        return carry

    lax.fori_loop(0, channels, resample, 0)
    group = basis_ref.shape[0] // channels
    owned = sent_ref.shape[2]

    for index in range(rows // group):
        block = resampled_ref[:, index * group : (index + 1) * group, :].reshape(
            channels * group, width
        )
        coefficients = jnp.dot(
            analysis_ref[...], block, preferred_element_type=jnp.float32
        ).astype(jnp.bfloat16)
        model = jnp.dot(basis_ref[...], coefficients, preferred_element_type=jnp.float32)
        residual = (block.astype(jnp.float32) - model).reshape(
            channels, group // owned, owned, width
        )
        for part in range(group // owned):
            sent_ref[index * (group // owned) + part] = residual[:, part].astype(jnp.bfloat16)


def combine_kernel(weights_ref, values_ref, map_ref):
    total, channels = values_ref.shape[0], values_ref.shape[1]

    def one(channel, carry):
        mean_level = values_ref[0, channel].astype(jnp.float32)
        for index in range(1, total):
            mean_level = mean_level + values_ref[index, channel].astype(jnp.float32)
        mean_level = mean_level / total
        spread = jnp.zeros_like(mean_level)
        weighted = jnp.zeros_like(mean_level)
        for index in range(total):
            deviation = values_ref[index, channel].astype(jnp.float32) - mean_level
            spread = spread + deviation * deviation
            weighted = weighted + weights_ref[index] * deviation
        spread = spread / total + 1e-05
        map_ref[channel] = weighted / jnp.sqrt(total * spread)
        return carry

    lax.fori_loop(0, channels, one, 0)


def body(
    exposures,
    fake_flux,
    fake_rows,
    fake_cols,
    kernel_taps,
    band_offsets,
    analysis,
    spectral_basis,
    exposure_weights,
):
    _, channels, local_rows, width = exposures.shape
    row_parts = lax.axis_size("row")
    exp_parts = lax.axis_size("exp")
    owned_rows = local_rows * row_parts // exp_parts
    taps = kernel_taps.astype(jnp.bfloat16).astype(jnp.float32)
    first = pl.pallas_call(
        columns_kernel,
        out_shape=jax.ShapeDtypeStruct((row_parts, channels, local_rows, BLOCK), jnp.bfloat16),
        in_specs=[SMEM, SMEM, SMEM, SMEM, SMEM, VMEM],
        out_specs=VMEM,
        scratch_shapes=[pltpu.VMEM((channels, local_rows, width), jnp.bfloat16)],
        name="columns",
    )(fake_rows, fake_cols, band_offsets, taps, fake_flux, exposures[0])
    columns = lax.all_to_all(first, "row", split_axis=0, concat_axis=0, tiled=True)
    same = jnp.eye(local_rows, dtype=jnp.bfloat16)
    residual = pl.pallas_call(
        rows_kernel,
        out_shape=jax.ShapeDtypeStruct((exp_parts, channels, owned_rows, BLOCK), jnp.bfloat16),
        in_specs=[SMEM, SMEM, VMEM, VMEM, VMEM],
        out_specs=VMEM,
        scratch_shapes=[pltpu.VMEM((channels, local_rows * row_parts, BLOCK), jnp.bfloat16)],
        name="rows",
    )(band_offsets, taps, jnp.kron(analysis, same), jnp.kron(spectral_basis, same), columns)
    gathered = lax.all_to_all(residual, "exp", split_axis=0, concat_axis=0, tiled=True)
    return pl.pallas_call(
        combine_kernel,
        out_shape=jax.ShapeDtypeStruct((channels, owned_rows, BLOCK), jnp.float32),
        in_specs=[SMEM, VMEM],
        out_specs=VMEM,
        name="combine",
    )(exposure_weights, gathered)


def solution(mesh):
    return jax.shard_map(
        body,
        mesh=mesh,
        in_specs=(
            P("exp", None, "row", None),
            P("exp", None, None),
            P(),
            P(),
            P(),
            P(),
            P(),
            P(),
            P(),
        ),
        out_specs=P(None, "exp", "row"),
        check_vma=False,
    )
```

```python
import functools

import jax
import jax.numpy as jnp
from jax import lax
from jax.experimental import pallas as pl
from jax.experimental.pallas import tpu as pltpu
from jax.sharding import PartitionSpec as P


LANES = 128
NEAR = 64
GROUPS = 3
RING = 4
GRANT = 20 * 2**20
VMEM = pl.BlockSpec(memory_space=pltpu.VMEM)
SMEM = pl.BlockSpec(memory_space=pltpu.SMEM)
ANY = pl.BlockSpec(memory_space=pl.ANY)
HBM = pl.BlockSpec(memory_space=pltpu.HBM)


def circulant(taps_ref, offsets_ref, channel, sign):
    lane = lax.broadcasted_iota(jnp.int32, (8, LANES), 1)
    signed = jnp.where(lane < NEAR, lane, lane - LANES)
    place = sign * signed - offsets_ref[channel]
    values = jnp.zeros((8, LANES), jnp.float32)
    for tap_index in range(taps_ref.shape[0]):
        values = jnp.where(place == tap_index, taps_ref[tap_index, channel], values)
    rows = jnp.concatenate([values] * (LANES // 8), axis=0)
    return pltpu.roll(rows, 0, 1, stride=1, stride_axis=0)


def partner(me, step, sign):
    return (me // RING ^ step // RING) * RING + (me + sign * step) % RING


def gaps():
    inner = lax.broadcasted_iota(jnp.int32, (LANES, LANES), 0)
    outer = lax.broadcasted_iota(jnp.int32, (LANES, LANES), 1)
    return jnp.abs(outer - inner)


def inject(rows_ref, cols_ref, flux_ref, held_ref, first_channel, channels):
    local_rows = held_ref.shape[1]
    row_start = lax.axis_index("row") * local_rows
    count = rows_ref.shape[0]

    def one(which, carry):
        row, column = rows_ref[which], cols_ref[which]
        local = row - row_start

        @pl.when((local >= 0) & (local < local_rows))
        def _():
            def look(other, counts):
                same = (rows_ref[other] == row) & (cols_ref[other] == column)
                return (
                    counts[0] + jnp.where(same & (other < which), 1, 0),
                    counts[1] + jnp.where(same & (other > which), 1, 0),
                )

            earlier, later = lax.fori_loop(0, count, look, (jnp.int32(0), jnp.int32(0)))
            start = pl.multiple_of((column // LANES) * LANES, LANES)
            row_ids = lax.broadcasted_iota(jnp.int32, (local_rows, LANES), 0)
            col_ids = lax.broadcasted_iota(jnp.int32, (local_rows, LANES), 1)
            hit = (row_ids == local) & (col_ids == column - start)

            def add(channel, total):
                tile = held_ref[channel, :, pl.ds(start, LANES)].astype(jnp.float32)
                held_ref[channel, :, pl.ds(start, LANES)] = jnp.where(
                    hit, tile + total, tile
                ).astype(jnp.bfloat16)

            @pl.when((earlier == 0) & (later == 0))
            def _():
                for index in range(channels):
                    channel = first_channel + index
                    add(channel, flux_ref[0, which, channel])

            @pl.when((earlier == 0) & (later > 0))
            def _():
                def shared(index, inner):
                    channel = first_channel + index

                    def gather(other, total):
                        same = (rows_ref[other] == row) & (cols_ref[other] == column)
                        return total + jnp.where(same, flux_ref[0, other, channel], 0.0)

                    add(channel, lax.fori_loop(0, count, gather, jnp.float32(0.0)))
                    return inner

                lax.fori_loop(0, channels, shared, 0)

        return carry

    lax.fori_loop(0, count, one, 0)


def columns_kernel(half, count, rows_ref, cols_ref, offsets_ref, taps_ref, flux_ref, frames_ref, *refs):
    sent_refs, (held_ref, done_ref, in_sems, out_sems) = refs[:count], refs[count:]
    channels, local_rows, width = held_ref.shape
    size = channels // GROUPS
    blocks = width // LANES

    def load(group):
        span = pl.ds(group * size, size)
        return pltpu.make_async_copy(frames_ref.at[span], held_ref.at[span], in_sems.at[group])

    def saves(group):
        span = pl.ds(group * size, size)
        if count == 1:
            pairs = [(done_ref.at[:, span], sent_refs[0].at[:, span])]
        else:
            me = lax.axis_index("row")
            pairs = [
                (done_ref.at[partner(me, step, 1), span], sent_refs[step].at[span])
                for step in range(count)
            ]
        return [
            pltpu.make_async_copy(source, target, out_sems.at[group, step])
            for step, (source, target) in enumerate(pairs)
        ]

    for group in range(GROUPS):
        load(group).start()
    gap = gaps()
    lane = lax.broadcasted_iota(jnp.int32, (local_rows, LANES), 1)
    edge = jnp.zeros((local_rows, LANES), jnp.bfloat16)

    def work(group, carry):
        load(group).wait()
        inject(rows_ref, cols_ref, flux_ref, held_ref, group * size, size)
        for index in range(size):
            channel = group * size + index
            ring = circulant(taps_ref, offsets_ref, channel, -1)
            weights = jnp.concatenate(
                [
                    jnp.where(gap < NEAR, ring, 0.0).astype(jnp.bfloat16),
                    jnp.where(gap >= NEAR, ring, 0.0).astype(jnp.bfloat16),
                ],
                axis=0,
            )
            lines = []
            for block in range(half, blocks, 2):
                start = block * LANES
                here = held_ref[channel, :, start : start + LANES]
                after = held_ref[channel, :, start + LANES : start + 2 * LANES] if block < blocks - 1 else edge
                before = held_ref[channel, :, start - LANES : start] if block > 0 else edge
                lines.append(
                    jnp.concatenate([here, jnp.where(lane < NEAR, after, before)], axis=1)
                )
            result = jnp.dot(
                jnp.concatenate(lines, axis=0), weights, preferred_element_type=jnp.float32
            ).astype(jnp.bfloat16)
            for piece in range(blocks // 2):
                done_ref[piece, channel] = result[piece * local_rows : (piece + 1) * local_rows]
        for copy in saves(group):
            copy.start()
        return carry

    lax.fori_loop(0, GROUPS, work, 0)
    for group in range(GROUPS):
        for copy in saves(group):
            copy.wait()


def prepare_kernel(offsets_ref, taps_ref, analysis_ref, basis_ref, band_ref, wide_ref, tall_ref):
    channels = band_ref.shape[0]
    size = channels // GROUPS
    gap = gaps()

    def work(group, carry):
        for index in range(size):
            channel = group * size + index
            ring = circulant(taps_ref, offsets_ref, channel, 1)
            band_ref[channel] = jnp.where(gap < NEAR, ring, 0.0).astype(jnp.bfloat16)
        return carry

    lax.fori_loop(0, GROUPS, work, 0)
    rank = analysis_ref.shape[0]
    short, long = wide_ref.shape
    rows = short // rank

    def onehot(shape, dim):
        left = lax.broadcasted_iota(jnp.int32, shape, dim) // rows
        return (left == lax.broadcasted_iota(jnp.int32, shape, 1 - dim)).astype(jnp.bfloat16)

    def contract(left, right, dims):
        return lax.dot_general(
            left, right, ((dims[:1], dims[1:]), ((), ())), preferred_element_type=jnp.float32
        ).astype(jnp.bfloat16)

    upper = contract(
        contract(onehot((short, rank), 0), analysis_ref[...], (1, 0)),
        onehot((channels, long), 1),
        (1, 0),
    )
    keep = (
        lax.broadcasted_iota(jnp.int32, (short, long), 0) % rows
        == lax.broadcasted_iota(jnp.int32, (short, long), 1) % rows
    )
    wide_ref[...] = jnp.where(keep, upper.astype(jnp.float32), 0.0).astype(jnp.bfloat16)
    lower = contract(
        contract(onehot((long, channels), 0), basis_ref[...], (1, 1)),
        onehot((rank, short), 1),
        (1, 0),
    )
    keep = (
        lax.broadcasted_iota(jnp.int32, (long, short), 0) % rows
        == lax.broadcasted_iota(jnp.int32, (long, short), 1) % rows
    )
    tall_ref[...] = jnp.where(keep, lower.astype(jnp.float32), 0.0).astype(jnp.bfloat16)


def rows_kernel(count, wide_ref, tall_ref, band_ref, *refs):
    columns_refs, refs = refs[:count], refs[count:]
    sent_ref, bands_ref, held_ref, resampled_ref, done_ref, band_sems, in_sems, out_sems = refs
    parts, channels, part_rows, width = held_ref.shape
    rows = parts * part_rows
    size = channels // GROUPS

    def load(group):
        span = pl.ds(group * size, size)
        if count == 1:
            pairs = [(columns_refs[0].at[:, span], held_ref.at[:, span])]
        else:
            me = lax.axis_index("row")
            pairs = [
                (columns_refs[step].at[span], held_ref.at[partner(me, step, -1), span])
                for step in range(count)
            ]
        return [
            pltpu.make_async_copy(band_ref.at[span], bands_ref.at[span], band_sems.at[group])
        ] + [
            pltpu.make_async_copy(source, target, in_sems.at[group, step])
            for step, (source, target) in enumerate(pairs)
        ]

    for group in range(GROUPS):
        for copy in load(group):
            copy.start()

    def work(group, carry):
        for copy in load(group):
            copy.wait()
        for index in range(size):
            channel = group * size + index
            resampled_ref[channel] = jnp.dot(
                bands_ref[channel],
                held_ref[:, channel].reshape(rows, width),
                preferred_element_type=jnp.float32,
            ).astype(jnp.bfloat16)
        return carry

    lax.fori_loop(0, GROUPS, work, 0)
    owned = done_ref.shape[2]
    long = tall_ref.shape[0]
    steps = rows // (2 * part_rows)
    each = 2 * part_rows // owned

    def save(step):
        span = pl.ds(step * each, each)
        return pltpu.make_async_copy(done_ref.at[span], sent_ref.at[span], out_sems.at[step])

    for step in range(steps):
        start = step * 2 * part_rows
        block = jnp.concatenate(
            [
                resampled_ref[:, start : start + part_rows, :].reshape(long, width),
                resampled_ref[:, start + part_rows : start + 2 * part_rows, :].reshape(long, width),
            ],
            axis=1,
        )
        coefficients = jnp.dot(
            wide_ref[...], block, preferred_element_type=jnp.float32
        ).astype(jnp.bfloat16)
        model = jnp.dot(tall_ref[...], coefficients, preferred_element_type=jnp.float32)
        residual = block.astype(jnp.float32) - model
        for side in range(2):
            values = residual[:, side * width : (side + 1) * width].reshape(
                channels, part_rows // owned, owned, width
            )
            for part in range(part_rows // owned):
                done_ref[step * each + side * (part_rows // owned) + part] = values[
                    :, part
                ].astype(jnp.bfloat16)
        save(step).start()
    for step in range(steps):
        save(step).wait()


def combine_kernel(weights_ref, values_ref, *refs):
    map_ref = refs[-1]
    total, channels = values_ref.shape[0], values_ref.shape[1]
    for channel in range(channels):
        values = [values_ref[index, channel].astype(jnp.float32) for index in range(total)]
        sums = values
        while len(sums) > 1:
            sums = [left + right for left, right in zip(sums[::2], sums[1::2])]
        mean_level = sums[0] / total
        spread = jnp.zeros_like(mean_level)
        weighted = jnp.zeros_like(mean_level)
        for index in range(total):
            deviation = values[index] - mean_level
            spread = spread + deviation * deviation
            weighted = weighted + weights_ref[index] * deviation
        spread = spread / total + 1e-05
        map_ref[channel] = weighted / jnp.sqrt(total * spread)


def estimate(flops, moved):
    return pl.CostEstimate(flops=flops, bytes_accessed=moved, transcendentals=0)


def program(
    exposures,
    fake_flux,
    fake_rows,
    fake_cols,
    kernel_taps,
    band_offsets,
    analysis,
    spectral_basis,
    exposure_weights,
):
    _, channels, local_rows, width = exposures.shape
    row_parts = lax.axis_size("row")
    exp_parts = lax.axis_size("exp")
    rows = local_rows * row_parts
    owned = rows // exp_parts
    rank = analysis.shape[0]
    taps = kernel_taps.T
    flux = jnp.swapaxes(fake_flux, 1, 2)
    half_shape = (row_parts, channels, local_rows, LANES)
    out_shape = (exp_parts, channels, owned, LANES)
    bf16 = jnp.bfloat16
    dma = pltpu.SemaphoreType.DMA

    def resample_columns(half, count):
        shape = half_shape if count == 1 else half_shape[1:]
        return pl.pallas_call(
            functools.partial(columns_kernel, half, count),
            out_shape=[jax.ShapeDtypeStruct(shape, bf16)] * count,
            in_specs=[SMEM] * 5 + [ANY],
            out_specs=[ANY] * count,
            scratch_shapes=[
                pltpu.VMEM((channels, local_rows, width), bf16),
                pltpu.VMEM(half_shape, bf16),
                dma((GROUPS,)),
                dma((GROUPS, count)),
            ],
            cost_estimate=estimate(10**9, 4 * 10**6),
        )(fake_rows, fake_cols, band_offsets, taps, flux, exposures[0])

    def resample_rows(band, wide, tall, columns):
        count = len(columns)
        return pl.pallas_call(
            functools.partial(rows_kernel, count),
            out_shape=jax.ShapeDtypeStruct(out_shape, bf16),
            in_specs=[VMEM, VMEM, HBM] + [ANY] * count,
            out_specs=HBM,
            scratch_shapes=[
                pltpu.VMEM((channels, rows, rows), bf16),
                pltpu.VMEM(half_shape, bf16),
                pltpu.VMEM((channels, rows, LANES), bf16),
                pltpu.VMEM(out_shape, bf16),
                dma((GROUPS,)),
                dma((GROUPS, count)),
                dma((row_parts // 2,)),
            ],
            compiler_params=pltpu.CompilerParams(vmem_limit_bytes=GRANT),
            cost_estimate=estimate(10**9, 4 * 10**6),
        )(wide, tall, band, *columns)

    def combine(half, gathered, *started):
        size = channels // GROUPS
        return pl.pallas_call(
            combine_kernel,
            grid=(GROUPS,),
            out_shape=jax.ShapeDtypeStruct((channels, owned, 2 * LANES), jnp.float32),
            in_specs=[
                SMEM,
                pl.BlockSpec((exp_parts, size, owned, LANES), lambda step: (0, step, 0, 0)),
            ]
            + [ANY] * len(started),
            out_specs=pl.BlockSpec((size, owned, LANES), lambda step: (step, 0, half)),
            input_output_aliases={2: 0} if started else {},
            compiler_params=pltpu.CompilerParams(vmem_limit_bytes=GRANT),
            cost_estimate=estimate(10**7, 2 * 10**6),
        )(exposure_weights, gathered, *started)

    band, wide, tall = pl.pallas_call(
        prepare_kernel,
        out_shape=[
            jax.ShapeDtypeStruct((channels, rows, rows), bf16),
            jax.ShapeDtypeStruct((rank * local_rows, channels * local_rows), bf16),
            jax.ShapeDtypeStruct((channels * local_rows, rank * local_rows), bf16),
        ],
        in_specs=[SMEM, SMEM, VMEM, VMEM],
        out_specs=[VMEM] * 3,
        cost_estimate=estimate(10**7, 2 * 10**6),
        name="prepare",
    )(band_offsets, taps, analysis, spectral_basis.T)

    def exchange(value, axis):
        return lax.all_to_all(value, axis, split_axis=0, concat_axis=0, tiled=True)

    def shift(value, step):
        if step == 0:
            return value
        pairs = [(me, int(partner(me, step, 1))) for me in range(row_parts)]
        return lax.ppermute(value, "row", pairs)

    (first,) = resample_columns(0, 1)
    columns = [[exchange(first, "row")]]
    pieces = resample_columns(1, row_parts)
    columns.append([shift(value, step) for step, value in enumerate(pieces)])
    residual = [resample_rows(band, wide, tall, columns[half]) for half in range(2)]
    gathered = [exchange(value, "exp") for value in residual]
    return combine(1, gathered[1], combine(0, gathered[0]))


def solution(mesh):
    return jax.shard_map(
        program,
        mesh=mesh,
        in_specs=(
            P("exp", None, "row", None),
            P("exp", None, None),
            P(),
            P(),
            P(),
            P(),
            P(),
            P(),
            P(),
        ),
        out_specs=P(None, "exp", "row"),
        check_vma=False,
    )
```

```python
import functools

import jax
import jax.numpy as jnp
from jax import lax
from jax.experimental import pallas as pl
from jax.experimental.pallas import tpu as pltpu
from jax.sharding import PartitionSpec as P


LANES = 128
NEAR = 64
GROUPS = 3
RING = 4
GRANT = 20 * 2**20
VMEM = pl.BlockSpec(memory_space=pltpu.VMEM)
SMEM = pl.BlockSpec(memory_space=pltpu.SMEM)
ANY = pl.BlockSpec(memory_space=pl.ANY)
HBM = pl.BlockSpec(memory_space=pltpu.HBM)


def circulant(taps_ref, offsets_ref, channel, sign):
    lane = lax.broadcasted_iota(jnp.int32, (8, LANES), 1)
    signed = jnp.where(lane < NEAR, lane, lane - LANES)
    place = sign * signed - offsets_ref[channel]
    values = jnp.zeros((8, LANES), jnp.float32)
    for tap_index in range(taps_ref.shape[0]):
        values = jnp.where(place == tap_index, taps_ref[tap_index, channel], values)
    rows = jnp.concatenate([values] * (LANES // 8), axis=0)
    return pltpu.roll(rows, 0, 1, stride=1, stride_axis=0)


def partner(me, step, sign):
    return (me // RING ^ step // RING) * RING + (me + sign * step) % RING


def chip_partner(chip, step, sign):
    return (chip // 2 + sign * (step // 2)) % RING * 2 + (chip % 2 ^ step % 2)


def gaps():
    inner = lax.broadcasted_iota(jnp.int32, (LANES, LANES), 0)
    outer = lax.broadcasted_iota(jnp.int32, (LANES, LANES), 1)
    return jnp.abs(outer - inner)


def find_local(rows_ref, cols_ref, list_ref, kind_ref, local_rows):
    row_start = lax.axis_index("row") * local_rows

    def look(which, found):
        local = rows_ref[which] - row_start
        list_ref[found] = which
        return found + jnp.where((local >= 0) & (local < local_rows), 1, 0)

    found = lax.fori_loop(0, rows_ref.shape[0], look, jnp.int32(0))

    def sort(place, carry):
        row, column = rows_ref[list_ref[place]], cols_ref[list_ref[place]]

        def compare(other, counts):
            which = list_ref[other]
            same = (rows_ref[which] == row) & (cols_ref[which] == column)
            return (
                counts[0] + jnp.where(same & (other < place), 1, 0),
                counts[1] + jnp.where(same & (other > place), 1, 0),
            )

        earlier, later = lax.fori_loop(0, found, compare, (jnp.int32(0), jnp.int32(0)))
        kind_ref[place] = jnp.where(earlier > 0, 0, jnp.where(later > 0, 2, 1))
        return carry

    lax.fori_loop(0, found, sort, 0)
    return found


def inject(
    found, list_ref, kind_ref, rows_ref, cols_ref, flux_ref, held_ref, first_channel, channels
):
    local_rows = held_ref.shape[1]
    row_start = lax.axis_index("row") * local_rows

    def one(place, carry):
        which, kind = list_ref[place], kind_ref[place]
        row, column = rows_ref[which], cols_ref[which]
        start = pl.multiple_of((column // LANES) * LANES, LANES)
        row_ids = lax.broadcasted_iota(jnp.int32, (local_rows, LANES), 0)
        col_ids = lax.broadcasted_iota(jnp.int32, (local_rows, LANES), 1)
        hit = (row_ids == row - row_start) & (col_ids == column - start)

        def add(channel, total):
            tile = held_ref[channel, :, pl.ds(start, LANES)].astype(jnp.float32)
            held_ref[channel, :, pl.ds(start, LANES)] = jnp.where(
                hit, tile + total, tile
            ).astype(jnp.bfloat16)

        @pl.when(kind == 1)
        def _():
            for index in range(channels):
                channel = first_channel + index
                add(channel, flux_ref[0, which, channel])

        @pl.when(kind == 2)
        def _():
            def shared(index, inner):
                channel = first_channel + index

                def gather(other, total):
                    same = (rows_ref[other] == row) & (cols_ref[other] == column)
                    return total + jnp.where(same, flux_ref[0, other, channel], 0.0)

                add(channel, lax.fori_loop(0, rows_ref.shape[0], gather, jnp.float32(0.0)))
                return inner

            lax.fori_loop(0, channels, shared, 0)

        return carry

    lax.fori_loop(0, found, one, 0)


def columns_kernel(half, count, rows_ref, cols_ref, flux_ref, frames_ref, *refs):
    if half == 0:
        (offsets_ref, taps_ref), refs = refs[:2], refs[2:]
        ring_in_ref = None
    else:
        ring_in_ref, refs = refs[0], refs[1:]
    sent_refs, refs = refs[:count], refs[count:]
    if half == 0:
        ring_out_ref, refs = refs[0], refs[1:]
    held_ref, done_ref, ring_ref, list_ref, kind_ref, in_sems, out_sems, ring_sems = refs
    channels, local_rows, width = held_ref.shape
    size = channels // GROUPS
    blocks = width // LANES

    def loads(group):
        span = pl.ds(group * size, size)
        copies = [
            pltpu.make_async_copy(frames_ref.at[span], held_ref.at[span], in_sems.at[group])
        ]
        if half == 1:
            copies.append(
                pltpu.make_async_copy(
                    ring_in_ref.at[span], ring_ref.at[span], ring_sems.at[group]
                )
            )
        return copies

    def saves(group):
        span = pl.ds(group * size, size)
        if count == 1:
            pairs = [(done_ref.at[:, span], sent_refs[0].at[:, span])]
        else:
            me = lax.axis_index("row")
            pairs = [
                (done_ref.at[partner(me, step, 1), span], sent_refs[step].at[span])
                for step in range(count)
            ]
        copies = [
            pltpu.make_async_copy(source, target, out_sems.at[group, step])
            for step, (source, target) in enumerate(pairs)
        ]
        if half == 0:
            copies.append(
                pltpu.make_async_copy(
                    ring_ref.at[span], ring_out_ref.at[span], ring_sems.at[group]
                )
            )
        return copies

    for group in range(GROUPS):
        for copy in loads(group):
            copy.start()
    found = find_local(rows_ref, cols_ref, list_ref, kind_ref, local_rows)
    gap = gaps()
    lane = lax.broadcasted_iota(jnp.int32, (local_rows, LANES), 1)
    edge = jnp.zeros((local_rows, LANES), jnp.bfloat16)

    def work(group, carry):
        for copy in loads(group):
            copy.wait()
        inject(
            found,
            list_ref,
            kind_ref,
            rows_ref,
            cols_ref,
            flux_ref,
            held_ref,
            group * size,
            size,
        )
        for index in range(size):
            channel = group * size + index
            if half == 0:
                ring = circulant(taps_ref, offsets_ref, channel, -1).astype(jnp.bfloat16)
                ring_ref[channel] = ring
            else:
                ring = ring_ref[channel]
            weights = jnp.concatenate(
                [
                    jnp.where(gap < NEAR, ring, jnp.zeros_like(ring)),
                    jnp.where(gap >= NEAR, ring, jnp.zeros_like(ring)),
                ],
                axis=0,
            )
            lines = []
            for block in range(half, blocks, 2):
                start = block * LANES
                here = held_ref[channel, :, start : start + LANES]
                after = held_ref[channel, :, start + LANES : start + 2 * LANES] if block < blocks - 1 else edge
                before = held_ref[channel, :, start - LANES : start] if block > 0 else edge
                lines.append(
                    jnp.concatenate([here, jnp.where(lane < NEAR, after, before)], axis=1)
                )
            result = jnp.dot(
                jnp.concatenate(lines, axis=0), weights, preferred_element_type=jnp.float32
            ).astype(jnp.bfloat16)
            for piece in range(blocks // 2):
                done_ref[piece, channel] = result[piece * local_rows : (piece + 1) * local_rows]
        for copy in saves(group):
            copy.start()
        return carry

    lax.fori_loop(0, GROUPS, work, 0)
    for group in range(GROUPS):
        for copy in saves(group):
            copy.wait()


def prepare_kernel(offsets_ref, taps_ref, analysis_ref, basis_ref, band_ref, wide_ref, tall_ref):
    channels = band_ref.shape[0]
    size = channels // GROUPS
    gap = gaps()

    def work(group, carry):
        for index in range(size):
            channel = group * size + index
            ring = circulant(taps_ref, offsets_ref, channel, 1)
            band_ref[channel] = jnp.where(gap < NEAR, ring, 0.0).astype(jnp.bfloat16)
        return carry

    lax.fori_loop(0, GROUPS, work, 0)
    rank = analysis_ref.shape[0]
    short, long = wide_ref.shape
    rows = short // rank

    def onehot(shape, dim):
        left = lax.broadcasted_iota(jnp.int32, shape, dim) // rows
        return (left == lax.broadcasted_iota(jnp.int32, shape, 1 - dim)).astype(jnp.bfloat16)

    def contract(left, right, dims):
        return lax.dot_general(
            left, right, ((dims[:1], dims[1:]), ((), ())), preferred_element_type=jnp.float32
        ).astype(jnp.bfloat16)

    upper = contract(
        contract(onehot((short, rank), 0), analysis_ref[...], (1, 0)),
        onehot((channels, long), 1),
        (1, 0),
    )
    keep = (
        lax.broadcasted_iota(jnp.int32, (short, long), 0) % rows
        == lax.broadcasted_iota(jnp.int32, (short, long), 1) % rows
    )
    wide_ref[...] = jnp.where(keep, upper.astype(jnp.float32), 0.0).astype(jnp.bfloat16)
    lower = contract(
        contract(onehot((long, channels), 0), basis_ref[...], (1, 1)),
        onehot((rank, short), 1),
        (1, 0),
    )
    keep = (
        lax.broadcasted_iota(jnp.int32, (long, short), 0) % rows
        == lax.broadcasted_iota(jnp.int32, (long, short), 1) % rows
    )
    tall_ref[...] = jnp.where(keep, lower.astype(jnp.float32), 0.0).astype(jnp.bfloat16)


def rows_kernel(count, chips, wide_ref, tall_ref, band_ref, *refs):
    columns_refs, refs = refs[:count], refs[count:]
    sent_refs, refs = refs[:chips], refs[chips:]
    held_ref, resampled_ref, done_ref, out_sems = refs
    parts, channels, part_rows, width = resampled_ref.shape
    size = channels // GROUPS
    if count > 1:
        me = lax.axis_index("row")
        for step in range(count):
            held_ref[partner(me, step, -1)] = columns_refs[step][...]
        values_ref = held_ref
    else:
        values_ref = columns_refs[0]

    def work(group, carry):
        for index in range(size):
            channel = group * size + index
            result = jnp.dot(
                band_ref[channel],
                values_ref[:, channel].reshape(parts * part_rows, width),
                preferred_element_type=jnp.float32,
            ).astype(jnp.bfloat16)
            for part in range(parts):
                resampled_ref[part, channel] = result[part * part_rows : (part + 1) * part_rows]
        return carry

    lax.fori_loop(0, GROUPS, work, 0)
    owned = done_ref.shape[2]
    long = tall_ref.shape[0]
    steps = parts // 2
    each = 2 * part_rows // owned
    mine = lax.axis_index("exp") // 2

    def save(step):
        span = pl.ds(step * each, each)
        return pltpu.make_async_copy(done_ref.at[span], sent_refs[0].at[span], out_sems.at[step])

    for step in range(steps):
        if chips == 1:
            places = [2 * step, 2 * step + 1]
        else:
            places = [chip_partner(mine, 2 * step + side, 1) for side in range(2)]
        block = jnp.concatenate(
            [resampled_ref[place].reshape(long, width) for place in places], axis=1
        )
        coefficients = jnp.dot(
            wide_ref[...], block, preferred_element_type=jnp.float32
        ).astype(jnp.bfloat16)
        model = jnp.dot(tall_ref[...], coefficients, preferred_element_type=jnp.float32)
        residual = block.astype(jnp.float32) - model
        for side in range(2):
            values = residual[:, side * width : (side + 1) * width].reshape(
                channels, part_rows // owned, owned, width
            )
            for part in range(part_rows // owned):
                piece = values[:, part].astype(jnp.bfloat16)
                if chips == 1:
                    done_ref[step * each + side * (part_rows // owned) + part] = piece
                else:
                    sent_refs[2 * step + side][part] = piece
        if chips == 1:
            save(step).start()
    if chips == 1:
        for step in range(steps):
            save(step).wait()


def forward_kernel(*refs):
    given, kept_ref = refs[:-1], refs[-1]
    other = 1 - lax.axis_index("exp") % 2
    for index, ref in enumerate(given):
        kept_ref[index] = ref[other]


def combine_channel(sources, channel):
    total = len(sources)
    values = [ref[index, channel].astype(jnp.float32) for ref, index, _ in sources]
    sums = values
    while len(sums) > 1:
        sums = [left + right for left, right in zip(sums[::2], sums[1::2])]
    mean_level = sums[0] / total
    spread = jnp.zeros_like(mean_level)
    weighted = jnp.zeros_like(mean_level)
    for value, (_, _, weight) in zip(values, sources):
        deviation = value - mean_level
        spread = spread + deviation * deviation
        weighted = weighted + weight * deviation
    spread = spread / total + 1e-05
    return weighted / jnp.sqrt(total * spread)


def combine_kernel(weights_ref, values_ref, map_ref):
    channels = map_ref.shape[0]
    size = channels // GROUPS
    sources = [
        (values_ref, index, weights_ref[index]) for index in range(values_ref.shape[0])
    ]

    def work(group, carry):
        for index in range(size):
            map_ref[group * size + index] = combine_channel(sources, group * size + index)
        return carry

    lax.fori_loop(0, GROUPS, work, 0)


def finish_kernel(weights_ref, first_ref, swapped_ref, *refs):
    kept_refs, (map_ref, held_ref, sems) = refs[:-3], refs[-3:]
    channels = held_ref.shape[0]
    size = channels // GROUPS
    me = lax.axis_index("exp")
    core = me % 2
    sources = []
    for step, ref in enumerate(kept_refs):
        chip = chip_partner(me // 2, step, -1)
        sources.append((ref, core, weights_ref[2 * chip + core]))
        sources.append((swapped_ref, step, weights_ref[2 * chip + 1 - core]))

    def save(group):
        span = pl.ds(group * size, size)
        return pltpu.make_async_copy(held_ref.at[span], map_ref.at[span], sems.at[group])

    def work(group, carry):
        for index in range(size):
            channel = group * size + index
            held_ref[channel, :, :LANES] = first_ref[channel]
            held_ref[channel, :, LANES:] = combine_channel(sources, channel)
        save(group).start()
        return carry

    lax.fori_loop(0, GROUPS, work, 0)
    for group in range(GROUPS):
        save(group).wait()


def estimate(flops, moved):
    return pl.CostEstimate(flops=flops, bytes_accessed=moved, transcendentals=0)


def program(
    exposures,
    fake_flux,
    fake_rows,
    fake_cols,
    kernel_taps,
    band_offsets,
    analysis,
    spectral_basis,
    exposure_weights,
):
    _, channels, local_rows, width = exposures.shape
    row_parts = lax.axis_size("row")
    exp_parts = lax.axis_size("exp")
    rows = local_rows * row_parts
    owned = rows // exp_parts
    rank = analysis.shape[0]
    taps = kernel_taps.T
    flux = jnp.swapaxes(fake_flux, 1, 2)
    half_shape = (row_parts, channels, local_rows, LANES)
    out_shape = (exp_parts, channels, owned, LANES)
    bf16 = jnp.bfloat16
    dma = pltpu.SemaphoreType.DMA

    def resample_columns(half, count, *weights):
        shape = half_shape if count == 1 else half_shape[1:]
        square = (channels, LANES, LANES)
        rings = 1 if half == 0 else 0
        return pl.pallas_call(
            functools.partial(columns_kernel, half, count),
            out_shape=[jax.ShapeDtypeStruct(shape, bf16)] * count
            + [jax.ShapeDtypeStruct(square, bf16)] * rings,
            in_specs=[SMEM] * 3 + [ANY] + ([SMEM] * 2 if half == 0 else [ANY]),
            out_specs=[ANY] * (count + rings),
            scratch_shapes=[
                pltpu.VMEM((channels, local_rows, width), bf16),
                pltpu.VMEM(half_shape, bf16),
                pltpu.VMEM(square, bf16),
                pltpu.SMEM((fake_rows.shape[0] + 1,), jnp.int32),
                pltpu.SMEM((fake_rows.shape[0] + 1,), jnp.int32),
                dma((GROUPS,)),
                dma((GROUPS, count)),
                dma((GROUPS,)),
            ],
            cost_estimate=estimate(10**9, 4 * 10**6),
        )(fake_rows, fake_cols, flux, exposures[0], *weights)

    def resample_rows(chips, band, wide, tall, columns):
        count = len(columns)
        shape = (exp_parts // chips,) + out_shape[1:]
        return pl.pallas_call(
            functools.partial(rows_kernel, count, chips),
            out_shape=[jax.ShapeDtypeStruct(shape, bf16)] * chips,
            in_specs=[VMEM] * (3 + count),
            out_specs=[ANY if chips == 1 else VMEM] * chips,
            scratch_shapes=[
                pltpu.VMEM(half_shape, bf16),
                pltpu.VMEM(half_shape, bf16),
                pltpu.VMEM(out_shape, bf16),
                dma((row_parts // 2,)),
            ],
            compiler_params=pltpu.CompilerParams(vmem_limit_bytes=GRANT),
            cost_estimate=estimate(10**9, 4 * 10**6),
        )(wide, tall, band, *columns)

    def forward(given):
        return pl.pallas_call(
            forward_kernel,
            out_shape=jax.ShapeDtypeStruct((len(given),) + out_shape[1:], bf16),
            in_specs=[VMEM] * len(given),
            out_specs=VMEM,
            compiler_params=pltpu.CompilerParams(vmem_limit_bytes=GRANT),
            cost_estimate=estimate(0, 2 * 10**6),
            name="forward",
        )(*given)

    def combine(gathered):
        return pl.pallas_call(
            combine_kernel,
            out_shape=jax.ShapeDtypeStruct(out_shape[1:], jnp.float32),
            in_specs=[SMEM, VMEM],
            out_specs=VMEM,
            compiler_params=pltpu.CompilerParams(vmem_limit_bytes=GRANT),
            cost_estimate=estimate(10**7, 2 * 10**6),
            name="combine",
        )(exposure_weights, gathered)

    def finish(first, swapped, kept):
        shape = (channels, owned, 2 * LANES)
        return pl.pallas_call(
            finish_kernel,
            out_shape=jax.ShapeDtypeStruct(shape, jnp.float32),
            in_specs=[SMEM] + [VMEM] * (2 + len(kept)),
            out_specs=ANY,
            scratch_shapes=[pltpu.VMEM(shape, jnp.float32), dma((GROUPS,))],
            compiler_params=pltpu.CompilerParams(vmem_limit_bytes=GRANT),
            cost_estimate=estimate(10**7, 2 * 10**6),
            name="finish",
        )(exposure_weights, first, swapped, *kept)

    band, wide, tall = pl.pallas_call(
        prepare_kernel,
        out_shape=[
            jax.ShapeDtypeStruct((channels, rows, rows), bf16),
            jax.ShapeDtypeStruct((rank * local_rows, channels * local_rows), bf16),
            jax.ShapeDtypeStruct((channels * local_rows, rank * local_rows), bf16),
        ],
        in_specs=[SMEM, SMEM, VMEM, VMEM],
        out_specs=[VMEM] * 3,
        compiler_params=pltpu.CompilerParams(vmem_limit_bytes=GRANT),
        cost_estimate=estimate(10**7, 2 * 10**6),
        name="prepare",
    )(band_offsets, taps, analysis, spectral_basis.T)

    def exchange(value, axis):
        return lax.all_to_all(value, axis, split_axis=0, concat_axis=0, tiled=True)

    def shift(value, step):
        if step == 0:
            return value
        pairs = [(me, int(partner(me, step, 1))) for me in range(row_parts)]
        return lax.ppermute(value, "row", pairs)

    first, ring = resample_columns(0, 1, band_offsets, taps)
    columns = [[exchange(first, "row")]]
    pieces = resample_columns(1, row_parts, ring)
    columns.append([shift(value, step) for step, value in enumerate(pieces)])
    (residual,) = resample_rows(1, band, wide, tall, columns[0])
    gathered = exchange(residual, "exp")
    pieces = resample_rows(exp_parts // 2, band, wide, tall, columns[1])

    def pass_on(value, step):
        if step == 0:
            return value
        pairs = [
            (me, int(chip_partner(me // 2, step, 1)) * 2 + me % 2) for me in range(exp_parts)
        ]
        return lax.ppermute(value, "exp", pairs)

    kept = [pass_on(value, step) for step, value in enumerate(pieces)]
    swapped = lax.ppermute(forward(kept), "exp", [(me, me ^ 1) for me in range(exp_parts)])
    return finish(combine(gathered), swapped, kept)


def solution(mesh):
    return jax.shard_map(
        program,
        mesh=mesh,
        in_specs=(
            P("exp", None, "row", None),
            P("exp", None, None),
            P(),
            P(),
            P(),
            P(),
            P(),
            P(),
            P(),
        ),
        out_specs=P(None, "exp", "row"),
        check_vma=False,
    )
```

```python
import functools

import jax
import jax.numpy as jnp
from jax import lax
from jax.experimental import pallas as pl
from jax.experimental.pallas import tpu as pltpu
from jax.sharding import PartitionSpec as P


LANES = 128
NEAR = 64
GROUPS = 3
RING = 4
ROW_ORDER = (4, 1, 3, 6, 5, 7, 2, 0)
CHIP_ORDER = (5, 4, 3, 7, 2, 6, 1, 0)
GRANT = 8 * 2**20
VMEM = pl.BlockSpec(memory_space=pltpu.VMEM)
SMEM = pl.BlockSpec(memory_space=pltpu.SMEM)
ANY = pl.BlockSpec(memory_space=pl.ANY)
HBM = pl.BlockSpec(memory_space=pltpu.HBM)


def circulant(taps_ref, offsets_ref, channel, sign):
    lane = lax.broadcasted_iota(jnp.int32, (8, LANES), 1)
    signed = jnp.where(lane < NEAR, lane, lane - LANES)
    place = sign * signed - offsets_ref[channel]
    values = jnp.zeros((8, LANES), jnp.float32)
    for tap_index in range(taps_ref.shape[0]):
        values = jnp.where(place == tap_index, taps_ref[tap_index, channel], values)
    rows = jnp.concatenate([values] * (LANES // 8), axis=0)
    return pltpu.roll(rows, 0, 1, stride=1, stride_axis=0)


def partner(me, step, sign):
    step = ROW_ORDER[step]
    return (me // RING ^ step // RING) * RING + (me + sign * step) % RING


def chip_partner(chip, step, sign):
    step = CHIP_ORDER[step]
    return (chip // 2 + sign * (step // 2)) % RING * 2 + (chip % 2 ^ step % 2)


def gaps():
    inner = lax.broadcasted_iota(jnp.int32, (LANES, LANES), 0)
    outer = lax.broadcasted_iota(jnp.int32, (LANES, LANES), 1)
    return jnp.abs(outer - inner)


def find_local(rows_ref, cols_ref, list_ref, kind_ref, local_rows):
    row_start = lax.axis_index("row") * local_rows

    def look(which, found):
        local = rows_ref[which] - row_start
        list_ref[found] = which
        return found + jnp.where((local >= 0) & (local < local_rows), 1, 0)

    found = lax.fori_loop(0, rows_ref.shape[0], look, jnp.int32(0))

    def sort(place, carry):
        row, column = rows_ref[list_ref[place]], cols_ref[list_ref[place]]

        def compare(other, counts):
            which = list_ref[other]
            same = (rows_ref[which] == row) & (cols_ref[which] == column)
            return (
                counts[0] + jnp.where(same & (other < place), 1, 0),
                counts[1] + jnp.where(same & (other > place), 1, 0),
            )

        earlier, later = lax.fori_loop(0, found, compare, (jnp.int32(0), jnp.int32(0)))
        kind_ref[place] = jnp.where(earlier > 0, 0, jnp.where(later > 0, 2, 1))
        return carry

    lax.fori_loop(0, found, sort, 0)
    return found


def inject(
    found, list_ref, kind_ref, rows_ref, cols_ref, flux_ref, held_ref, first_channel, channels
):
    local_rows = held_ref.shape[1]
    row_start = lax.axis_index("row") * local_rows

    def one(place, carry):
        which, kind = list_ref[place], kind_ref[place]
        row, column = rows_ref[which], cols_ref[which]
        start = pl.multiple_of((column // LANES) * LANES, LANES)
        row_ids = lax.broadcasted_iota(jnp.int32, (local_rows, LANES), 0)
        col_ids = lax.broadcasted_iota(jnp.int32, (local_rows, LANES), 1)
        hit = (row_ids == row - row_start) & (col_ids == column - start)

        def add(channel, total):
            tile = held_ref[channel, :, pl.ds(start, LANES)].astype(jnp.float32)
            held_ref[channel, :, pl.ds(start, LANES)] = jnp.where(
                hit, tile + total, tile
            ).astype(jnp.bfloat16)

        @pl.when(kind == 1)
        def _():
            for index in range(channels):
                channel = first_channel + index
                add(channel, flux_ref[0, which, channel])

        @pl.when(kind == 2)
        def _():
            def shared(index, inner):
                channel = first_channel + index

                def gather(other, total):
                    same = (rows_ref[other] == row) & (cols_ref[other] == column)
                    return total + jnp.where(same, flux_ref[0, other, channel], 0.0)

                add(channel, lax.fori_loop(0, rows_ref.shape[0], gather, jnp.float32(0.0)))
                return inner

            lax.fori_loop(0, channels, shared, 0)

        return carry

    lax.fori_loop(0, found, one, 0)


def columns_kernel(half, count, rows_ref, cols_ref, flux_ref, frames_ref, *refs):
    if half == 0:
        (offsets_ref, taps_ref), refs = refs[:2], refs[2:]
        ring_in_ref = None
    else:
        ring_in_ref, refs = refs[0], refs[1:]
    sent_refs, refs = refs[:count], refs[count:]
    if half == 0:
        ring_out_ref, refs = refs[0], refs[1:]
    held_ref, done_ref, ring_ref, list_ref, kind_ref, in_sems, out_sems, ring_sems = refs
    channels, local_rows, width = held_ref.shape
    size = channels // GROUPS
    blocks = width // LANES

    def loads(group):
        span = pl.ds(group * size, size)
        copies = [
            pltpu.make_async_copy(frames_ref.at[span], held_ref.at[span], in_sems.at[group])
        ]
        if half == 1:
            copies.append(
                pltpu.make_async_copy(
                    ring_in_ref.at[span], ring_ref.at[span], ring_sems.at[group]
                )
            )
        return copies

    def saves(group):
        span = pl.ds(group * size, size)
        if count == 1:
            pairs = [(done_ref.at[:, span], sent_refs[0].at[:, span])]
        else:
            me = lax.axis_index("row")
            pairs = [
                (done_ref.at[partner(me, step, 1), span], sent_refs[step].at[span])
                for step in range(count)
            ]
        copies = [
            pltpu.make_async_copy(source, target, out_sems.at[group, step])
            for step, (source, target) in enumerate(pairs)
        ]
        if half == 0:
            copies.append(
                pltpu.make_async_copy(
                    ring_ref.at[span], ring_out_ref.at[span], ring_sems.at[group]
                )
            )
        return copies

    for group in range(GROUPS):
        for copy in loads(group):
            copy.start()
    found = find_local(rows_ref, cols_ref, list_ref, kind_ref, local_rows)
    gap = gaps()
    lane = lax.broadcasted_iota(jnp.int32, (local_rows, LANES), 1)
    edge = jnp.zeros((local_rows, LANES), jnp.bfloat16)

    def work(group, carry):
        for copy in loads(group):
            copy.wait()
        inject(
            found,
            list_ref,
            kind_ref,
            rows_ref,
            cols_ref,
            flux_ref,
            held_ref,
            group * size,
            size,
        )
        for index in range(size):
            channel = group * size + index
            if half == 0:
                ring = circulant(taps_ref, offsets_ref, channel, -1).astype(jnp.bfloat16)
                ring_ref[channel] = ring
            else:
                ring = ring_ref[channel]
            weights = jnp.concatenate(
                [
                    jnp.where(gap < NEAR, ring, jnp.zeros_like(ring)),
                    jnp.where(gap >= NEAR, ring, jnp.zeros_like(ring)),
                ],
                axis=0,
            )
            lines = []
            for block in range(half, blocks, 2):
                start = block * LANES
                here = held_ref[channel, :, start : start + LANES]
                after = held_ref[channel, :, start + LANES : start + 2 * LANES] if block < blocks - 1 else edge
                before = held_ref[channel, :, start - LANES : start] if block > 0 else edge
                lines.append(
                    jnp.concatenate([here, jnp.where(lane < NEAR, after, before)], axis=1)
                )
            result = jnp.dot(
                jnp.concatenate(lines, axis=0), weights, preferred_element_type=jnp.float32
            ).astype(jnp.bfloat16)
            for piece in range(blocks // 2):
                done_ref[piece, channel] = result[piece * local_rows : (piece + 1) * local_rows]
        for copy in saves(group):
            copy.start()
        return carry

    for group in range(GROUPS):
        work(group, 0)
    for group in range(GROUPS):
        for copy in saves(group):
            copy.wait()


def prepare_kernel(offsets_ref, taps_ref, analysis_ref, basis_ref, band_ref, wide_ref, tall_ref):
    channels = band_ref.shape[0]
    size = channels // GROUPS
    gap = gaps()

    def work(group, carry):
        for index in range(size):
            channel = group * size + index
            ring = circulant(taps_ref, offsets_ref, channel, 1)
            band_ref[channel] = jnp.where(gap < NEAR, ring, 0.0).astype(jnp.bfloat16)
        return carry

    lax.fori_loop(0, GROUPS, work, 0)
    rank = analysis_ref.shape[0]
    short, long = wide_ref.shape
    rows = short // rank

    def onehot(shape, dim):
        left = lax.broadcasted_iota(jnp.int32, shape, dim) // rows
        return (left == lax.broadcasted_iota(jnp.int32, shape, 1 - dim)).astype(jnp.bfloat16)

    def contract(left, right, dims):
        return lax.dot_general(
            left, right, ((dims[:1], dims[1:]), ((), ())), preferred_element_type=jnp.float32
        ).astype(jnp.bfloat16)

    upper = contract(
        contract(onehot((short, rank), 0), analysis_ref[...], (1, 0)),
        onehot((channels, long), 1),
        (1, 0),
    )
    keep = (
        lax.broadcasted_iota(jnp.int32, (short, long), 0) % rows
        == lax.broadcasted_iota(jnp.int32, (short, long), 1) % rows
    )
    wide_ref[...] = jnp.where(keep, upper.astype(jnp.float32), 0.0).astype(jnp.bfloat16)
    lower = contract(
        contract(onehot((long, channels), 0), basis_ref[...], (1, 1)),
        onehot((rank, short), 1),
        (1, 0),
    )
    keep = (
        lax.broadcasted_iota(jnp.int32, (long, short), 0) % rows
        == lax.broadcasted_iota(jnp.int32, (long, short), 1) % rows
    )
    tall_ref[...] = jnp.where(keep, lower.astype(jnp.float32), 0.0).astype(jnp.bfloat16)


def rows_kernel(count, chips, wide_ref, tall_ref, band_ref, *refs):
    columns_refs, refs = refs[:count], refs[count:]
    sent_refs, refs = refs[:chips], refs[chips:]
    held_ref, resampled_ref, done_ref, out_sems = refs
    parts, channels, part_rows, width = resampled_ref.shape
    size = channels // GROUPS
    if count > 1:
        me = lax.axis_index("row")
        for step in range(count):
            held_ref[partner(me, step, -1)] = columns_refs[step][...]
        values_ref = held_ref
    else:
        values_ref = columns_refs[0]

    def work(group, carry):
        for index in range(size):
            channel = group * size + index
            result = jnp.dot(
                band_ref[channel],
                values_ref[:, channel].reshape(parts * part_rows, width),
                preferred_element_type=jnp.float32,
            ).astype(jnp.bfloat16)
            for part in range(parts):
                resampled_ref[part, channel] = result[part * part_rows : (part + 1) * part_rows]
        return carry

    for group in range(GROUPS):
        work(group, 0)
    owned = done_ref.shape[2]
    long = tall_ref.shape[0]
    steps = parts // 2
    each = 2 * part_rows // owned
    mine = lax.axis_index("exp") // 2

    def save(step):
        span = pl.ds(step * each, each)
        return pltpu.make_async_copy(done_ref.at[span], sent_refs[0].at[span], out_sems.at[step])

    for step in range(steps):
        if chips == 1:
            places = [2 * step, 2 * step + 1]
        else:
            places = [chip_partner(mine, 2 * step + side, 1) for side in range(2)]
        block = jnp.concatenate(
            [resampled_ref[place].reshape(long, width) for place in places], axis=1
        )
        coefficients = jnp.dot(
            wide_ref[...], block, preferred_element_type=jnp.float32
        ).astype(jnp.bfloat16)
        model = jnp.dot(tall_ref[...], coefficients, preferred_element_type=jnp.float32)
        residual = block.astype(jnp.float32) - model
        for side in range(2):
            values = residual[:, side * width : (side + 1) * width].reshape(
                channels, part_rows // owned, owned, width
            )
            for part in range(part_rows // owned):
                piece = values[:, part].astype(jnp.bfloat16)
                if chips == 1:
                    done_ref[step * each + side * (part_rows // owned) + part] = piece
                else:
                    sent_refs[2 * step + side][part] = piece
        if chips == 1:
            save(step).start()
    if chips == 1:
        for step in range(steps):
            save(step).wait()


def forward_kernel(*refs):
    given, (own_ref, other_ref) = refs[:-2], refs[-2:]
    core = lax.axis_index("exp") % 2
    for index, ref in enumerate(given):
        own_ref[index] = ref[core]
        other_ref[index] = ref[1 - core]


def combine_channel(sources, channel):
    total = len(sources)
    values = [ref[index, channel].astype(jnp.float32) for ref, index, _ in sources]
    sums = values
    while len(sums) > 1:
        sums = [left + right for left, right in zip(sums[::2], sums[1::2])]
    mean_level = sums[0] / total
    spread = jnp.zeros_like(mean_level)
    weighted = jnp.zeros_like(mean_level)
    for value, (_, _, weight) in zip(values, sources):
        deviation = value - mean_level
        spread = spread + deviation * deviation
        weighted = weighted + weight * deviation
    spread = spread / total + 1e-05
    return weighted / jnp.sqrt(total * spread)


def sources_of(weights_ref, refs):
    if len(refs) == 1:
        return [(refs[0], index, weights_ref[index]) for index in range(refs[0].shape[0])]
    me = lax.axis_index("exp")
    sources = []
    for step in range(refs[0].shape[0]):
        chip = chip_partner(me // 2, step, -1)
        sources.append((refs[0], step, weights_ref[2 * chip + me % 2]))
        sources.append((refs[1], step, weights_ref[2 * chip + 1 - me % 2]))
    return sources


def combine_kernel(weights_ref, *refs):
    values_refs, map_ref = refs[:-1], refs[-1]
    size = map_ref.shape[0] // GROUPS
    sources = sources_of(weights_ref, values_refs)

    def work(group, carry):
        for index in range(size):
            map_ref[group * size + index] = combine_channel(sources, group * size + index)
        return carry

    lax.fori_loop(0, GROUPS, work, 0)


def finish_kernel(other_half, weights_ref, ready_ref, *refs):
    values_refs, (map_ref, held_ref, sems) = refs[:-3], refs[-3:]
    size = held_ref.shape[0] // GROUPS
    sources = sources_of(weights_ref, values_refs)
    columns = [slice(0, LANES), slice(LANES, 2 * LANES)]

    def save(group):
        span = pl.ds(group * size, size)
        return pltpu.make_async_copy(held_ref.at[span], map_ref.at[span], sems.at[group])

    def work(group, carry):
        for index in range(size):
            channel = group * size + index
            held_ref[channel, :, columns[other_half]] = ready_ref[channel]
            held_ref[channel, :, columns[1 - other_half]] = combine_channel(sources, channel)
        save(group).start()
        return carry

    lax.fori_loop(0, GROUPS, work, 0)
    for group in range(GROUPS):
        save(group).wait()


def estimate(flops, moved):
    return pl.CostEstimate(flops=flops, bytes_accessed=moved, transcendentals=0)


def program(
    exposures,
    fake_flux,
    fake_rows,
    fake_cols,
    kernel_taps,
    band_offsets,
    analysis,
    spectral_basis,
    exposure_weights,
):
    _, channels, local_rows, width = exposures.shape
    row_parts = lax.axis_size("row")
    exp_parts = lax.axis_size("exp")
    rows = local_rows * row_parts
    owned = rows // exp_parts
    rank = analysis.shape[0]
    taps = kernel_taps.T
    flux = jnp.swapaxes(fake_flux, 1, 2)
    half_shape = (row_parts, channels, local_rows, LANES)
    out_shape = (exp_parts, channels, owned, LANES)
    bf16 = jnp.bfloat16
    dma = pltpu.SemaphoreType.DMA

    def resample_columns(half, count, *weights):
        shape = half_shape if count == 1 else half_shape[1:]
        square = (channels, LANES, LANES)
        rings = 1 if half == 0 else 0
        return pl.pallas_call(
            functools.partial(columns_kernel, half, count),
            out_shape=[jax.ShapeDtypeStruct(shape, bf16)] * count
            + [jax.ShapeDtypeStruct(square, bf16)] * rings,
            in_specs=[SMEM] * 3 + [ANY] + ([SMEM] * 2 if half == 0 else [ANY]),
            out_specs=[ANY] * (count + rings),
            scratch_shapes=[
                pltpu.VMEM((channels, local_rows, width), bf16),
                pltpu.VMEM(half_shape, bf16),
                pltpu.VMEM(square, bf16),
                pltpu.SMEM((fake_rows.shape[0] + 1,), jnp.int32),
                pltpu.SMEM((fake_rows.shape[0] + 1,), jnp.int32),
                dma((GROUPS,)),
                dma((GROUPS, count)),
                dma((GROUPS,)),
            ],
            cost_estimate=estimate(10**9, 4 * 10**6),
        )(fake_rows, fake_cols, flux, exposures[0], *weights)

    def resample_rows(chips, band, wide, tall, columns):
        count = len(columns)
        shape = (exp_parts // chips,) + out_shape[1:]
        return pl.pallas_call(
            functools.partial(rows_kernel, count, chips),
            out_shape=[jax.ShapeDtypeStruct(shape, bf16)] * chips,
            in_specs=[VMEM] * (3 + count),
            out_specs=[ANY if chips == 1 else VMEM] * chips,
            scratch_shapes=[
                pltpu.VMEM(half_shape, bf16),
                pltpu.VMEM(half_shape, bf16),
                pltpu.VMEM(out_shape, bf16),
                dma((row_parts // 2,)),
            ],
            compiler_params=pltpu.CompilerParams(vmem_limit_bytes=GRANT),
            cost_estimate=estimate(10**9, 4 * 10**6),
        )(wide, tall, band, *columns)

    def forward(given):
        return pl.pallas_call(
            forward_kernel,
            out_shape=[jax.ShapeDtypeStruct((len(given),) + out_shape[1:], bf16)] * 2,
            in_specs=[VMEM] * len(given),
            out_specs=[VMEM] * 2,
            compiler_params=pltpu.CompilerParams(vmem_limit_bytes=GRANT),
            cost_estimate=estimate(0, 2 * 10**6),
            name="forward",
        )(*given)

    def combine(*values):
        return pl.pallas_call(
            combine_kernel,
            out_shape=jax.ShapeDtypeStruct(out_shape[1:], jnp.float32),
            in_specs=[SMEM] + [VMEM] * len(values),
            out_specs=VMEM,
            compiler_params=pltpu.CompilerParams(vmem_limit_bytes=GRANT),
            cost_estimate=estimate(10**7, 2 * 10**6),
            name="combine",
        )(exposure_weights, *values)

    def finish(other_half, ready, *values):
        shape = (channels, owned, 2 * LANES)
        return pl.pallas_call(
            functools.partial(finish_kernel, other_half),
            out_shape=jax.ShapeDtypeStruct(shape, jnp.float32),
            in_specs=[SMEM] + [VMEM] * (1 + len(values)),
            out_specs=ANY,
            scratch_shapes=[pltpu.VMEM(shape, jnp.float32), dma((GROUPS,))],
            compiler_params=pltpu.CompilerParams(vmem_limit_bytes=GRANT),
            cost_estimate=estimate(10**7, 2 * 10**6),
            name="finish",
        )(exposure_weights, ready, *values)

    band, wide, tall = pl.pallas_call(
        prepare_kernel,
        out_shape=[
            jax.ShapeDtypeStruct((channels, rows, rows), bf16),
            jax.ShapeDtypeStruct((rank * local_rows, channels * local_rows), bf16),
            jax.ShapeDtypeStruct((channels * local_rows, rank * local_rows), bf16),
        ],
        in_specs=[SMEM, SMEM, VMEM, VMEM],
        out_specs=[VMEM] * 3,
        compiler_params=pltpu.CompilerParams(vmem_limit_bytes=GRANT),
        cost_estimate=estimate(10**7, 2 * 10**6),
        name="prepare",
    )(band_offsets, taps, analysis, spectral_basis.T)

    def exchange(value, axis):
        return lax.all_to_all(value, axis, split_axis=0, concat_axis=0, tiled=True)

    def shift(value, step):
        if ROW_ORDER[step] == 0:
            return value
        pairs = [(me, int(partner(me, step, 1))) for me in range(row_parts)]
        return lax.ppermute(value, "row", pairs)

    first, ring = resample_columns(0, 1, band_offsets, taps)
    columns = [[exchange(first, "row")]]
    pieces = resample_columns(1, row_parts, ring)
    columns.append([shift(value, step) for step, value in enumerate(pieces)])
    (residual,) = resample_rows(1, band, wide, tall, columns[0])
    gathered = exchange(residual, "exp")
    pieces = resample_rows(exp_parts // 2, band, wide, tall, columns[1])

    def pass_on(value, step):
        if CHIP_ORDER[step] == 0:
            return value
        pairs = [
            (me, int(chip_partner(me // 2, step, 1)) * 2 + me % 2) for me in range(exp_parts)
        ]
        return lax.ppermute(value, "exp", pairs)

    kept = [pass_on(value, step) for step, value in enumerate(pieces)]
    own, other = forward(kept)
    swapped = lax.ppermute(other, "exp", [(me, me ^ 1) for me in range(exp_parts)])
    return finish(0, combine(gathered), own, swapped)


def solution(mesh):
    return jax.shard_map(
        program,
        mesh=mesh,
        in_specs=(
            P("exp", None, "row", None),
            P("exp", None, None),
            P(),
            P(),
            P(),
            P(),
            P(),
            P(),
            P(),
        ),
        out_specs=P(None, "exp", "row"),
        check_vma=False,
    )
```
